32 devices in a mesh: shot: 16 (over z, x, core), freq: 2 (over y).
Axes of the slice: x: 2, y: 2, z: 4, core: 2. Of those that a mesh axis runs over, the one named last changes fastest.
Arguments:
- wavefield: bfloat16 [4, 6144, 1024], P('freq', 'shot'), parts along dimension 0, may hold values from -0.8984375 to 0.8984375
- recorded: bfloat16 [6, 2, 2, 6144, 384], P('freq', None, None, 'shot'), parts along dimension 0, may hold values from -6 to 6
- match_filter: bfloat16 [2, 63], replicated, may hold values from -0.5 to 0.5
Outputs:
- demultiple: bfloat16 [6, 2, 2, 6144, 384], P('freq', None, None, 'shot'), parts along dimension 0
The draws below stay inside these ranges and needn't reach their ends.
There are 2 independent parts, one for each index of `freq`. The reference program is written for one: setup_inputs(seed, part) draws one part's arguments, and reference() takes and returns one part's arrays. A program takes and returns all parts, laid end to end along the dimension named above; an argument that names none is the same for every part. Nothing has to cross between parts.
All inputs are finite; a program needn't handle non-finite values.
Results may differ from the reference program's by a relative error of at most 0.0048.
Values may be sent and summed in bfloat16 or wider, within the bound.
A program may use at most 64 MiB of HBM per device.

```python
import jax
import jax.numpy as jnp
from jax import lax

SHOT_DEV = 384
APERTURE = 1024
TAPS = 63
OFFSETS = 3
BLOCKS = 16
SHOTS = 6144


def block_scale(own_key, extent, pieces, smallest, high):
    def one(dim, blocks):
        steps = jax.random.uniform(jax.random.fold_in(jax.random.fold_in(own_key, 6), dim), (blocks,), jnp.float32, smallest / len(pieces), high / len(pieces))
        return jnp.repeat(jnp.exp(steps), extent[dim] // blocks).reshape((-1,) + (1,) * (len(extent) - dim - 1))

    gain = one(*pieces[0])
    for cut in pieces[1:]:
        gain = gain * one(*cut)
    return gain


def scatter_about(rng, shape, width, bound, pieces=(), kind=jnp.bfloat16):
    result = width * jax.random.normal(rng, shape, jnp.float32)
    if pieces:
        result = result * block_scale(rng, shape, pieces, -0.22, 0.18)
    return jnp.clip(result, -bound, bound).astype(kind)


def setup_inputs(seed: int = 0, part: int = 0) -> dict:
    streams_of = jax.random.split(jax.random.key(seed), 4)
    part_splits = jax.random.split(jax.random.fold_in(streams_of[3], part), 4)
    return {
        "wavefield": scatter_about(part_splits[0], (2, SHOTS, APERTURE), 0.15, 0.8984375, ((1, 16),)),
        "recorded": scatter_about(part_splits[1], (OFFSETS, 2, 2, SHOTS, SHOT_DEV), 1.0, 6.0, ((3, 16),)),
        "match_filter": scatter_about(streams_of[2], (2, TAPS), (2 * TAPS) ** -0.5, 0.5),
    }


def toeplitz(match_filter, block_span_width):
    tap_count = match_filter.shape[1]
    half_taps = (tap_count - 1) // 2
    row_index = lax.broadcasted_iota(jnp.int32, (block_span_width, block_span_width), 0)
    col_index = lax.broadcasted_iota(jnp.int32, (block_span_width, block_span_width), 1)
    lag_index = row_index - col_index + half_taps
    coeffs = match_filter.astype(jnp.float32)

    def place_tap(tap_index, carried):
        column = lax.dynamic_slice_in_dim(coeffs, tap_index, 1, 1)
        return jnp.where((lag_index == tap_index)[None], column[:, :, None], carried)

    return lax.fori_loop(0, tap_count, place_tap, jnp.zeros((2, block_span_width, block_span_width), jnp.float32))


def filter_weights(match_filter, block_span_width):
    toe_pair = toeplitz(match_filter, block_span_width)
    real_component = toe_pair[0].astype(jnp.bfloat16)
    imag_part = toe_pair[1].astype(jnp.bfloat16)
    return jnp.stack([jnp.stack([real_component, imag_part], 1), jnp.stack([-imag_part, real_component], 1)], 0)


def reference(wavefield, recorded, match_filter):
    weights = filter_weights(match_filter, SHOT_DEV).astype(jnp.float32)
    every_block = wavefield.astype(jnp.float32).reshape(2, BLOCKS, SHOT_DEV, APERTURE)
    outputs = []
    for slot_index, offset in enumerate((1, BLOCKS // 8, BLOCKS // 4)):
        paired_shot = jnp.roll(every_block, -offset, axis=1)
        real_block_tile = jnp.einsum("ldz,lez->lde", every_block[0], paired_shot[0]) - jnp.einsum("ldz,lez->lde", every_block[1], paired_shot[1])
        imaginary_tile = jnp.einsum("ldz,lez->lde", every_block[0], paired_shot[1]) + jnp.einsum("ldz,lez->lde", every_block[1], paired_shot[0])
        ahead_tiles = jnp.stack([real_block_tile, imaginary_tile], 1).astype(jnp.bfloat16)
        behind_tiles = jnp.swapaxes(jnp.roll(ahead_tiles, offset, axis=0), 2, 3)
        side_list = []
        for side_index, tile_set in enumerate((ahead_tiles, behind_tiles)):
            matched_output = jnp.einsum("bcsq,cqdx->dbsx", tile_set.astype(jnp.float32), weights)
            matched_output = matched_output.reshape(2, SHOTS, SHOT_DEV)
            side_list.append((recorded[slot_index, side_index].astype(jnp.float32) - matched_output).astype(jnp.bfloat16))
        outputs.append(jnp.stack(side_list))
    return jnp.stack(outputs)
```

```python
import functools

import jax
import jax.numpy as jnp
from jax import lax
from jax.experimental import pallas as pl
from jax.experimental.pallas import tpu as pltpu
from jax.sharding import PartitionSpec as P

MESH = pl.DeviceIdType.MESH
STEP = 128
CH_X, CH_Z, CH_M, CH_D, CH_A, CH_C, CH_O = range(7)
LIMIT = 40 * 2**20
F32 = jnp.float32
BF16 = jnp.bfloat16


def dot_t(a, b):
    return lax.dot_general(a, b, (((1,), (1,)), ((), ())), preferred_element_type=F32)


def kernel(
    n, mf_hbm, wave, rec, out,
    mf, wave_v, weights, buf_m, buf_c, buf_d, buf_z,
    send_a, send_c, send_x, recv_a, recv_c, recv_x, tile_m, tile_c, tile_z, tile_d,
    rec_v, res, taps_row,
    ssem, rsem, in_sem, out_sem,
):
    span, depth = wave_v.shape[1], wave_v.shape[2]
    pieces = span // STEP
    last = pieces - 1
    early = last * STEP
    cut = span // 2
    half = (mf.shape[1] - 1) // 2
    me = lax.axis_index("shot")
    core = lax.rem(me, 2)
    side = lax.rem(me // 2, 2)
    mate = me + 1 - 2 * core
    across = me + 2 - 4 * side
    cross = across + 1 - 2 * core
    up, down = lax.rem(me + 4, n), lax.rem(me + n - 4, n)
    z_to = (1 - side) * down + side * up
    z_from = (1 - side) * up + side * down
    owner = (core == side)
    giver = (core != side)

    load_taps = pltpu.make_async_copy(mf_hbm, mf, in_sem.at[2])
    load_taps.start()
    load_wave = pltpu.make_async_copy(wave, wave_v, in_sem.at[0])
    load_wave.start()
    load = pltpu.make_async_copy(rec, rec_v, in_sem.at[1])
    load.start()

    barrier = pltpu.get_barrier_semaphore()
    for other in (mate, across, cross, up, down):
        pl.semaphore_signal(barrier, inc=1, device_id={"shot": other}, device_id_type=MESH)
    pl.semaphore_wait(barrier, 5)

    def remote(src, dst, sem, target):
        return pltpu.make_async_remote_copy(
            src_ref=src, dst_ref=dst, send_sem=ssem.at[sem], recv_sem=rsem.at[sem],
            device_id={"shot": target}, device_id_type=MESH,
        )

    def block(src, dst, channel, i, target):
        rows = pl.ds(i * STEP, STEP)
        return remote(src.at[:, rows, :], dst.at[:, rows, :], channel * pieces + i, target)

    def x_copy(i):
        return block(wave, buf_c, CH_X, i, across)

    def z_copy(i):
        return block(wave, buf_z, CH_Z, i, z_to)

    def mate_copy(i):
        return block(wave, buf_m, CH_M, i, mate)

    def share(i):
        return block(buf_c, buf_d, CH_D, i, mate)

    def tile_a(i):
        return block(send_a, recv_a, CH_A, i, z_from)

    def corner(j):
        rows, cols = (
            (pl.ds(0, early), pl.ds(0, early)),
            (pl.ds(0, early), pl.ds(early, STEP)),
            (pl.ds(early, STEP), pl.ds(0, span)),
        )[j]
        return remote(
            send_c.at[:, rows, cols], recv_c.at[:, rows, cols], CH_C * pieces + j, across
        )

    def odd_x():
        rows = pl.ds(0, cut)
        return remote(send_x.at[:, rows, :], recv_x.at[:, rows, :], CH_O * pieces, cross)

    def odd_z():
        rows = pl.ds(cut, span - cut)
        return remote(send_x.at[:, rows, :], recv_x.at[:, rows, :], CH_O * pieces + 1, z_from)

    for i in range(pieces):
        x_copy(i).start()
        z_copy(i).start()
    for i in range(pieces):
        mate_copy(i).start()

    load_taps.wait()
    width = taps_row.shape[1]
    taps_row[...] = jnp.zeros_like(taps_row)
    taps_row[0:2, 0:mf.shape[1]] = mf[...].astype(F32)
    row_id = lax.broadcasted_iota(jnp.int32, (span, width), 0)
    banded = []
    for c in range(2):
        x = jnp.broadcast_to(taps_row[c:c + 1, :], (span, width))
        x = pltpu.roll(x, width - half, 1)
        bit = 1
        while bit < span:
            x = jnp.where((row_id // bit) % 2 == 1, pltpu.roll(x, bit, 1), x)
            bit *= 2
        banded.append(x[:, :span].astype(BF16))
    for j in range(pieces):
        a = banded[0][j * STEP:(j + 1) * STEP]
        b = banded[1][j * STEP:(j + 1) * STEP]
        at = 2 * j * STEP
        weights[0, at:at + STEP, :] = a
        weights[0, at + STEP:at + 2 * STEP, :] = b
        weights[1, at:at + STEP, :] = -b
        weights[1, at + STEP:at + 2 * STEP, :] = a

    def product(left, start, count, right, k):
        a = left[:, start:start + count, :].reshape(2 * count, depth)
        b = right[:, k * STEP:(k + 1) * STEP, :].reshape(2 * STEP, depth)
        y = dot_t(a, b)
        top, low = y[:count], y[count:]
        return top[:, :STEP] - low[:, STEP:], top[:, STEP:] + low[:, :STEP]

    def keep(dst, pair, start, count, k):
        for c in range(2):
            dst[c, start:start + count, k * STEP:(k + 1) * STEP] = pair[c].astype(BF16)

    def flipped(dst, pair, k, skip=0):
        for c in range(2):
            dst[c, k * STEP + skip:(k + 1) * STEP, :] = pair[c].T[skip:].astype(BF16)

    def put(t, k, start, count, j):
        rows = pl.ds(start, count)
        return pltpu.make_async_copy(
            res.at[t, k, :, rows, :], out.at[t, k, :, rows, :], out_sem.at[j]
        )

    def emit(t, k, src, start, count, j):
        rows = slice(start, start + count)
        for p in range(pieces):
            lo, hi = max(p - 1, 0) * STEP, min(p + 2, pieces) * STEP
            cols = slice(p * STEP, (p + 1) * STEP)
            f = sum(
                dot_t(src[c, rows, lo:hi], weights[c, 2 * p * STEP:2 * (p + 1) * STEP, lo:hi])
                for c in range(2)
            )
            res[t, k, 0, rows, cols] = (rec_v[t, k, 0, rows, cols].astype(F32) - f[:, :STEP]).astype(BF16)
            res[t, k, 1, rows, cols] = (rec_v[t, k, 1, rows, cols].astype(F32) - f[:, STEP:]).astype(BF16)
        put(t, k, start, count, j).start()

    load_wave.wait()
    for i in range(pieces):
        mate_copy(i).wait_recv()
        keep(tile_m, product(wave_v, 0, span, buf_m, i), 0, span, i)
    load.wait()
    emit(0, core, tile_m, 0, span, 0)

    for i in range(last):
        x_copy(i).wait_recv()
        share(i).start()
        keep(tile_c, product(wave_v, 0, span, buf_c, i), 0, span, i)
        z_copy(i).wait_recv()
        pair = product(wave_v, 0, span, buf_z, i)
        keep(tile_z, pair, 0, span, i)
        flipped(send_a, pair, i)
    for i in range(last):
        keep(send_c, product(buf_c, 0, early, buf_z, i), 0, early, i)
    corner(0).start()

    x_copy(last).wait_recv()
    share(last).start()
    z_copy(last).wait_recv()
    for i in range(last):
        tile_a(i).start()
    keep(send_c, product(buf_c, 0, early, buf_z, last), 0, early, last)
    corner(1).start()
    pair = product(wave_v, 0, span, buf_z, last)
    flipped(send_a, pair, last)
    tile_a(last).start()
    keep(tile_z, pair, 0, span, last)
    for i in range(pieces):
        keep(send_c, product(buf_c, early, STEP, buf_z, i), early, STEP, i)
    corner(2).start()

    for i in range(pieces):
        share(i).wait_recv()

    @pl.when(owner)
    def _():
        for i in range(pieces):
            pair = product(buf_d, 0, span, buf_z, i)
            for c in range(2):
                send_x[c, :cut, i * STEP:(i + 1) * STEP] = pair[c][:cut].astype(BF16)
            if (i + 1) * STEP > cut:
                flipped(send_x, pair, i, max(cut - i * STEP, 0))
        odd_x().start()
        odd_z().start()

    keep(tile_c, product(wave_v, 0, span, buf_c, last), 0, span, last)
    emit(1, side, tile_c, 0, span, 1)
    emit(2, side, tile_z, 0, span, 2)

    @pl.when(giver)
    def _():
        for i in range(pieces):
            keep(tile_d, product(wave_v, 0, span, buf_d, i), 0, span, i)
        emit(0, 1 - core, tile_d, 0, span, 3)

    corner(0).wait_recv()
    corner(1).wait_recv()
    emit(1, 1 - side, recv_c, 0, early, 4)
    for i in range(last):
        tile_a(i).wait_recv()
        emit(2, 1 - side, recv_a, i * STEP, STEP, 6 + i)
    corner(2).wait_recv()
    emit(1, 1 - side, recv_c, early, STEP, 5)
    tile_a(last).wait_recv()
    emit(2, 1 - side, recv_a, early, STEP, 6 + last)

    @pl.when(owner)
    def _():
        odd_x().wait_recv()
        emit(0, 1 - core, recv_x, 0, cut, 3)
        odd_z().wait_recv()
        emit(0, 1 - core, recv_x, cut, span - cut, 6 + pieces)
        odd_x().wait_send()
        odd_z().wait_send()
        put(0, 1 - core, 0, cut, 3).wait()
        put(0, 1 - core, cut, span - cut, 6 + pieces).wait()

    for i in range(pieces):
        x_copy(i).wait_send()
        z_copy(i).wait_send()
        mate_copy(i).wait_send()
        share(i).wait_send()
        tile_a(i).wait_send()
        put(2, 1 - side, i * STEP, STEP, 6 + i).wait()
    for j in range(3):
        corner(j).wait_send()
    put(0, core, 0, span, 0).wait()
    put(1, side, 0, span, 1).wait()
    put(2, side, 0, span, 2).wait()
    put(1, 1 - side, 0, early, 4).wait()
    put(1, 1 - side, early, STEP, 5).wait()

    @pl.when(giver)
    def _():
        put(0, 1 - core, 0, span, 3).wait()


def ladder(wavefield, recorded, match_filter):
    n = lax.axis_size("shot")
    _, span, depth = wavefield.shape
    pieces = span // STEP
    width = -(-(span + match_filter.shape[1]) // STEP) * STEP
    block = pltpu.VMEM((2, span, depth), BF16)
    flat = pltpu.VMEM((2, span, span), BF16)
    return pl.pallas_call(
        functools.partial(kernel, n),
        out_shape=jax.ShapeDtypeStruct(recorded.shape, recorded.dtype),
        in_specs=[
            pl.BlockSpec(memory_space=pltpu.HBM),
            pl.BlockSpec(memory_space=pltpu.HBM),
            pl.BlockSpec(memory_space=pltpu.HBM),
        ],
        out_specs=pl.BlockSpec(memory_space=pl.ANY),
        scratch_shapes=[
            pltpu.VMEM(match_filter.shape, BF16),
            block,
            pltpu.VMEM((2, 2 * span, span), BF16),
            block, block, block, block,
            flat, flat, flat, flat, flat, flat, flat, flat, flat, flat,
            pltpu.VMEM(recorded.shape, BF16),
            pltpu.VMEM(recorded.shape, BF16),
            pltpu.VMEM((8, width), F32),
            pltpu.SemaphoreType.DMA((7 * pieces,)),
            pltpu.SemaphoreType.DMA((7 * pieces,)),
            pltpu.SemaphoreType.DMA((3,)),
            pltpu.SemaphoreType.DMA((7 + pieces,)),
        ],
        compiler_params=pltpu.CompilerParams(
            collective_id=0, has_side_effects=True, vmem_limit_bytes=LIMIT
        ),
    )(*(pltpu.with_memory_space_constraint(x, pltpu.HBM) for x in (match_filter, wavefield, recorded)))


def passed_along(value, axis, steps):
    count = lax.axis_size(axis)
    pairs = [(source, (source + steps) % count) for source in range(count)]
    return lax.ppermute(value, axis, pairs)


def toeplitz(match_filter, block_span_width):
    tap_count = match_filter.shape[1]
    half_taps = (tap_count - 1) // 2
    row_index = lax.broadcasted_iota(jnp.int32, (block_span_width, block_span_width), 0)
    col_index = lax.broadcasted_iota(jnp.int32, (block_span_width, block_span_width), 1)
    lag_index = row_index - col_index + half_taps
    coeffs = match_filter.astype(jnp.float32)

    def place_tap(tap_index, carried):
        column = lax.dynamic_slice_in_dim(coeffs, tap_index, 1, 1)
        return jnp.where((lag_index == tap_index)[None], column[:, :, None], carried)

    return lax.fori_loop(
        0, tap_count, place_tap, jnp.zeros((2, block_span_width, block_span_width), jnp.float32)
    )


def filter_weights(match_filter, block_span_width):
    toe_pair = toeplitz(match_filter, block_span_width)
    real_component = toe_pair[0].astype(jnp.bfloat16)
    imag_part = toe_pair[1].astype(jnp.bfloat16)
    return jnp.stack(
        [jnp.stack([real_component, imag_part], 1), jnp.stack([-imag_part, real_component], 1)], 0
    )


def shards(wavefield, recorded, match_filter):
    cycle_size = lax.axis_size("shot")
    doubling = cycle_size // 8 == 2 and cycle_size // 4 == 4
    span, taps = wavefield.shape[1], match_filter.shape[1]
    tiled = span % STEP == 0 and span // STEP >= 3 and taps <= 2 * STEP and span % 32 == 0
    if doubling and cycle_size % 4 == 0 and tiled:
        return ladder(wavefield, recorded, match_filter)
    block_span_width = wavefield.shape[1]
    weights = filter_weights(match_filter, block_span_width)
    real_component = wavefield[0]
    imag_part = wavefield[1]
    left_rows = jnp.concatenate(
        [
            jnp.concatenate([real_component, -imag_part], 1),
            jnp.concatenate([imag_part, real_component], 1),
        ],
        0,
    )
    results = []
    for slot_index, offset in enumerate((1, cycle_size // 8, cycle_size // 4)):
        ahead_data = passed_along(wavefield, "shot", -offset)
        right_rows = jnp.concatenate([ahead_data[0], ahead_data[1]], 1)
        stacked = lax.dot_general(
            left_rows, right_rows, (((1,), (1,)), ((), ())), preferred_element_type=jnp.float32
        )
        forward_tile = stacked.astype(jnp.bfloat16).reshape(2, block_span_width, block_span_width)
        ahead_filtered = jnp.einsum(
            "csq,cqdx->dsx", forward_tile, weights, preferred_element_type=jnp.float32
        )
        received = passed_along(forward_tile, "shot", offset)
        behind_filtered = jnp.einsum(
            "csr,csdx->drx", received, weights, preferred_element_type=jnp.float32
        )
        ahead_out = (recorded[slot_index, 0].astype(jnp.float32) - ahead_filtered).astype(
            jnp.bfloat16
        )
        behind_out = (recorded[slot_index, 1].astype(jnp.float32) - behind_filtered).astype(
            jnp.bfloat16
        )
        results.append(jnp.stack([ahead_out, behind_out]))
    return jnp.stack(results)


def solution(mesh):
    return jax.shard_map(
        shards,
        mesh=mesh,
        in_specs=(P("freq", "shot", None), P("freq", None, None, "shot", None), P()),
        out_specs=P("freq", None, None, "shot", None),
        check_vma=False,
    )
```

```python
import functools

import jax
import jax.numpy as jnp
from jax import lax
from jax.experimental import pallas as pl
from jax.experimental.pallas import tpu as pltpu
from jax.sharding import PartitionSpec as P

MESH = pl.DeviceIdType.MESH
STEP = 128
HALF = STEP // 2
CH_X, CH_Z, CH_M, CH_D, CH_A, CH_C, CH_O = range(7)
LIMIT = 40 * 2**20
F32 = jnp.float32
BF16 = jnp.bfloat16


def dot_t(a, b):
    return lax.dot_general(a, b, (((1,), (1,)), ((), ())), preferred_element_type=F32)


def kernel(
    n, mf_hbm, wave, rec, out,
    mf, wave_v, weights, buf_m, buf_c, buf_d, buf_z,
    send_a, send_c, send_x, recv_a, recv_c, recv_x, tile_m, tile_c, tile_z, tile_d,
    rec_v, taps_row,
    ssem, rsem, in_sem,
):
    span, depth = wave_v.shape[1], wave_v.shape[2]
    pieces = span // STEP
    last = pieces - 1
    early = last * STEP
    cut = span // 2
    half = (mf.shape[1] - 1) // 2
    me = lax.axis_index("shot")
    core = lax.rem(me, 2)
    side = lax.rem(me // 2, 2)
    mate = me + 1 - 2 * core
    across = me + 2 - 4 * side
    cross = across + 1 - 2 * core
    up, down = lax.rem(me + 4, n), lax.rem(me + n - 4, n)
    z_to = (1 - side) * down + side * up
    z_from = (1 - side) * up + side * down
    deck = me // 4
    edge = (deck == 0) | (deck == n // 4 - 1)
    owner = (core == side)
    giver = (core != side)

    load_taps = pltpu.make_async_copy(mf_hbm, mf, in_sem.at[2])
    load_taps.start()
    load_wave = pltpu.make_async_copy(wave, wave_v, in_sem.at[0])
    load_wave.start()
    load = pltpu.make_async_copy(rec, rec_v, in_sem.at[1])
    load.start()

    barrier = pltpu.get_barrier_semaphore()
    for other in (mate, across, cross, up, down):
        pl.semaphore_signal(barrier, inc=1, device_id={"shot": other}, device_id_type=MESH)
    pl.semaphore_wait(barrier, 5)

    def remote(src, dst, sem, target):
        return pltpu.make_async_remote_copy(
            src_ref=src, dst_ref=dst, send_sem=ssem.at[sem], recv_sem=rsem.at[sem],
            device_id={"shot": target}, device_id_type=MESH,
        )

    def block(src, dst, channel, i, target):
        rows = pl.ds(i * STEP, STEP)
        return remote(src.at[:, rows, :], dst.at[:, rows, :], channel * pieces + i, target)

    def x_copy(i):
        return block(wave, buf_c, CH_X, i, across)

    def z_copy(i):
        return block(wave, buf_z, CH_Z, i, z_to)

    def z_half(j):
        rows = pl.ds(early + j * HALF, HALF)
        return remote(wave.at[:, rows, :], buf_z.at[:, rows, :], CH_Z * pieces + last if j == 0 else 7 * pieces, z_to)

    def mate_copy(i):
        return block(wave, buf_m, CH_M, i, mate)

    def share(i):
        return block(buf_c, buf_d, CH_D, i, mate)

    def tile_a(i):
        return block(send_a, recv_a, CH_A, i, z_from)

    def corner(j):
        rows, cols = (
            (pl.ds(0, early), pl.ds(0, early)),
            (pl.ds(0, early), pl.ds(early, STEP)),
            (pl.ds(early, STEP), pl.ds(0, span)),
        )[j]
        return remote(
            send_c.at[:, rows, cols], recv_c.at[:, rows, cols], CH_C * pieces + j, across
        )

    def odd_x():
        rows = pl.ds(0, cut)
        return remote(send_x.at[:, rows, :], recv_x.at[:, rows, :], CH_O * pieces, cross)

    def odd_z():
        rows = pl.ds(cut, span - cut)
        return remote(send_x.at[:, rows, :], recv_x.at[:, rows, :], CH_O * pieces + 1, z_from)

    for i in range(pieces):
        x_copy(i).start()
        if i < last:
            z_copy(i).start()
    z_half(0).start()
    z_half(1).start()
    for i in range(pieces):
        mate_copy(i).start()

    load_taps.wait()
    width = taps_row.shape[1]
    taps_row[...] = jnp.zeros_like(taps_row)
    taps_row[0:2, 0:mf.shape[1]] = mf[...].astype(F32)
    row_id = lax.broadcasted_iota(jnp.int32, (span, width), 0)
    banded = []
    for c in range(2):
        x = jnp.broadcast_to(taps_row[c:c + 1, :], (span, width))
        x = pltpu.roll(x, width - half, 1)
        bit = 1
        while bit < span:
            x = jnp.where((row_id // bit) % 2 == 1, pltpu.roll(x, bit, 1), x)
            bit *= 2
        banded.append(x[:, :span].astype(BF16))
    for j in range(pieces):
        a = banded[0][j * STEP:(j + 1) * STEP]
        b = banded[1][j * STEP:(j + 1) * STEP]
        at = 2 * j * STEP
        weights[0, at:at + STEP, :] = a
        weights[0, at + STEP:at + 2 * STEP, :] = b
        weights[1, at:at + STEP, :] = -b
        weights[1, at + STEP:at + 2 * STEP, :] = a

    def product(left, start, count, right, k):
        a = left[:, start:start + count, :].reshape(2 * count, depth)
        b = right[:, k * STEP:(k + 1) * STEP, :].reshape(2 * STEP, depth)
        y = dot_t(a, b)
        top, low = y[:count], y[count:]
        return top[:, :STEP] - low[:, STEP:], top[:, STEP:] + low[:, :STEP]

    def keep(dst, pair, start, count, k):
        for c in range(2):
            dst[c, start:start + count, k * STEP:(k + 1) * STEP] = pair[c].astype(BF16)

    def flipped(dst, pair, k, skip=0):
        for c in range(2):
            dst[c, k * STEP + skip:(k + 1) * STEP, :] = pair[c].T[skip:].astype(BF16)

    def emit(t, k, src, start, count, j):
        rows = slice(start, start + count)
        for p in range(pieces):
            lo, hi = max(p - 1, 0) * STEP, min(p + 2, pieces) * STEP
            cols = slice(p * STEP, (p + 1) * STEP)
            f = sum(
                dot_t(src[c, rows, lo:hi], weights[c, 2 * p * STEP:2 * (p + 1) * STEP, lo:hi])
                for c in range(2)
            )
            out[t, k, 0, rows, cols] = (rec_v[t, k, 0, rows, cols].astype(F32) - f[:, :STEP]).astype(BF16)
            out[t, k, 1, rows, cols] = (rec_v[t, k, 1, rows, cols].astype(F32) - f[:, STEP:]).astype(BF16)

    load_wave.wait()
    for i in range(pieces):
        mate_copy(i).wait_recv()
        keep(tile_m, product(wave_v, 0, span, buf_m, i), 0, span, i)
    load.wait()
    emit(0, core, tile_m, 0, span, 0)

    for i in range(last):
        x_copy(i).wait_recv()
        share(i).start()
        keep(tile_c, product(wave_v, 0, span, buf_c, i), 0, span, i)
        z_copy(i).wait_recv()
        pair = product(wave_v, 0, span, buf_z, i)
        keep(tile_z, pair, 0, span, i)
        flipped(send_a, pair, i)
        pl.when(edge)(tile_a(i).start)
    for i in range(last):
        keep(send_c, product(buf_c, 0, early, buf_z, i), 0, early, i)
    corner(0).start()

    x_copy(last).wait_recv()
    share(last).start()
    z_half(0).wait_recv()

    @pl.when(jnp.logical_not(edge))
    def _():
        for i in range(last):
            tile_a(i).start()

    z_half(1).wait_recv()
    keep(send_c, product(buf_c, 0, early, buf_z, last), 0, early, last)
    corner(1).start()
    pair = product(wave_v, 0, span, buf_z, last)
    flipped(send_a, pair, last)
    tile_a(last).start()
    keep(tile_z, pair, 0, span, last)
    for i in range(pieces):
        keep(send_c, product(buf_c, early, STEP, buf_z, i), early, STEP, i)
    corner(2).start()

    for i in range(pieces):
        share(i).wait_recv()

    @pl.when(owner)
    def _():
        for i in range(pieces):
            pair = product(buf_d, 0, span, buf_z, i)
            for c in range(2):
                send_x[c, :cut, i * STEP:(i + 1) * STEP] = pair[c][:cut].astype(BF16)
            if (i + 1) * STEP > cut:
                flipped(send_x, pair, i, max(cut - i * STEP, 0))
        odd_x().start()
        odd_z().start()

    keep(tile_c, product(wave_v, 0, span, buf_c, last), 0, span, last)
    emit(1, side, tile_c, 0, span, 1)
    emit(2, side, tile_z, 0, span, 2)

    @pl.when(giver)
    def _():
        for i in range(pieces):
            keep(tile_d, product(wave_v, 0, span, buf_d, i), 0, span, i)
        emit(0, 1 - core, tile_d, 0, span, 3)

    corner(0).wait_recv()
    corner(1).wait_recv()
    emit(1, 1 - side, recv_c, 0, early, 4)
    for i in range(last):
        tile_a(i).wait_recv()
        emit(2, 1 - side, recv_a, i * STEP, STEP, 6 + i)
    corner(2).wait_recv()
    emit(1, 1 - side, recv_c, early, STEP, 5)
    tile_a(last).wait_recv()
    emit(2, 1 - side, recv_a, early, STEP, 6 + last)

    @pl.when(owner)
    def _():
        odd_x().wait_recv()
        emit(0, 1 - core, recv_x, 0, cut, 3)
        odd_z().wait_recv()
        emit(0, 1 - core, recv_x, cut, span - cut, 6 + pieces)
        odd_x().wait_send()
        odd_z().wait_send()
        pass
        pass

    for i in range(pieces):
        x_copy(i).wait_send()
        if i < last:
            z_copy(i).wait_send()
        mate_copy(i).wait_send()
        share(i).wait_send()
        tile_a(i).wait_send()
        pass
    z_half(0).wait_send()
    z_half(1).wait_send()
    for j in range(3):
        corner(j).wait_send()
    pass
    pass
    pass
    pass
    pass

    @pl.when(giver)
    def _():
        pass


def ladder(wavefield, recorded, match_filter):
    n = lax.axis_size("shot")
    _, span, depth = wavefield.shape
    pieces = span // STEP
    width = -(-(span + match_filter.shape[1]) // STEP) * STEP
    block = pltpu.VMEM((2, span, depth), BF16)
    flat = pltpu.VMEM((2, span, span), BF16)
    return pl.pallas_call(
        functools.partial(kernel, n),
        out_shape=jax.ShapeDtypeStruct(recorded.shape, recorded.dtype),
        in_specs=[
            pl.BlockSpec(memory_space=pltpu.HBM),
            pl.BlockSpec(memory_space=pltpu.HBM),
            pl.BlockSpec(memory_space=pltpu.HBM),
        ],
        out_specs=pl.BlockSpec(memory_space=pltpu.VMEM),
        scratch_shapes=[
            pltpu.VMEM(match_filter.shape, BF16),
            block,
            pltpu.VMEM((2, 2 * span, span), BF16),
            block, block, block, block,
            flat, flat, flat, flat, flat, flat, flat, flat, flat, flat,
            pltpu.VMEM(recorded.shape, BF16),
            pltpu.VMEM((8, width), F32),
            pltpu.SemaphoreType.DMA((7 * pieces + 1,)),
            pltpu.SemaphoreType.DMA((7 * pieces + 1,)),
            pltpu.SemaphoreType.DMA((3,)),
        ],
        compiler_params=pltpu.CompilerParams(
            collective_id=0, has_side_effects=True, vmem_limit_bytes=LIMIT
        ),
    )(*(pltpu.with_memory_space_constraint(x, pltpu.HBM) for x in (match_filter, wavefield, recorded)))


def passed_along(value, axis, steps):
    count = lax.axis_size(axis)
    pairs = [(source, (source + steps) % count) for source in range(count)]
    return lax.ppermute(value, axis, pairs)


def toeplitz(match_filter, block_span_width):
    tap_count = match_filter.shape[1]
    half_taps = (tap_count - 1) // 2
    row_index = lax.broadcasted_iota(jnp.int32, (block_span_width, block_span_width), 0)
    col_index = lax.broadcasted_iota(jnp.int32, (block_span_width, block_span_width), 1)
    lag_index = row_index - col_index + half_taps
    coeffs = match_filter.astype(jnp.float32)

    def place_tap(tap_index, carried):
        column = lax.dynamic_slice_in_dim(coeffs, tap_index, 1, 1)
        return jnp.where((lag_index == tap_index)[None], column[:, :, None], carried)

    return lax.fori_loop(
        0, tap_count, place_tap, jnp.zeros((2, block_span_width, block_span_width), jnp.float32)
    )


def filter_weights(match_filter, block_span_width):
    toe_pair = toeplitz(match_filter, block_span_width)
    real_component = toe_pair[0].astype(jnp.bfloat16)
    imag_part = toe_pair[1].astype(jnp.bfloat16)
    return jnp.stack(
        [jnp.stack([real_component, imag_part], 1), jnp.stack([-imag_part, real_component], 1)], 0
    )


def shards(wavefield, recorded, match_filter):
    cycle_size = lax.axis_size("shot")
    doubling = cycle_size // 8 == 2 and cycle_size // 4 == 4
    span, taps = wavefield.shape[1], match_filter.shape[1]
    tiled = span % STEP == 0 and span // STEP >= 3 and taps <= 2 * STEP and span % 32 == 0
    if doubling and cycle_size % 4 == 0 and tiled:
        return ladder(wavefield, recorded, match_filter)
    block_span_width = wavefield.shape[1]
    weights = filter_weights(match_filter, block_span_width)
    real_component = wavefield[0]
    imag_part = wavefield[1]
    left_rows = jnp.concatenate(
        [
            jnp.concatenate([real_component, -imag_part], 1),
            jnp.concatenate([imag_part, real_component], 1),
        ],
        0,
    )
    results = []
    for slot_index, offset in enumerate((1, cycle_size // 8, cycle_size // 4)):
        ahead_data = passed_along(wavefield, "shot", -offset)
        right_rows = jnp.concatenate([ahead_data[0], ahead_data[1]], 1)
        stacked = lax.dot_general(
            left_rows, right_rows, (((1,), (1,)), ((), ())), preferred_element_type=jnp.float32
        )
        forward_tile = stacked.astype(jnp.bfloat16).reshape(2, block_span_width, block_span_width)
        ahead_filtered = jnp.einsum(
            "csq,cqdx->dsx", forward_tile, weights, preferred_element_type=jnp.float32
        )
        received = passed_along(forward_tile, "shot", offset)
        behind_filtered = jnp.einsum(
            "csr,csdx->drx", received, weights, preferred_element_type=jnp.float32
        )
        ahead_out = (recorded[slot_index, 0].astype(jnp.float32) - ahead_filtered).astype(
            jnp.bfloat16
        )
        behind_out = (recorded[slot_index, 1].astype(jnp.float32) - behind_filtered).astype(
            jnp.bfloat16
        )
        results.append(jnp.stack([ahead_out, behind_out]))
    return jnp.stack(results)


def solution(mesh):
    return jax.shard_map(
        shards,
        mesh=mesh,
        in_specs=(P("freq", "shot", None), P("freq", None, None, "shot", None), P()),
        out_specs=P("freq", None, None, "shot", None),
        check_vma=False,
    )
```

```python
import functools

import jax
import jax.numpy as jnp
from jax import lax
from jax.experimental import pallas as pl
from jax.experimental.pallas import tpu as pltpu
from jax.sharding import PartitionSpec as P

MESH = pl.DeviceIdType.MESH
STEP = 128
HALF = STEP // 2
CH_X, CH_Z, CH_M, CH_D, CH_A, CH_C, CH_O = range(7)
LIMIT = 40 * 2**20
F32 = jnp.float32
BF16 = jnp.bfloat16


def dot_t(a, b):
    return lax.dot_general(a, b, (((1,), (1,)), ((), ())), preferred_element_type=F32)


def kernel(
    n, mf_hbm, wave, rec, out,
    mf, wave_v, weights, buf_m, buf_c, buf_d, buf_z,
    send_a, send_c, send_x, recv_a, recv_c, recv_x, tile_m, tile_c, tile_z, tile_d,
    rec_v, taps_row,
    ssem, rsem, in_sem,
):
    span, depth = wave_v.shape[1], wave_v.shape[2]
    pieces = span // STEP
    last = pieces - 1
    early = last * STEP
    cut = span // 2
    half = (mf.shape[1] - 1) // 2
    me = lax.axis_index("shot")
    core = lax.rem(me, 2)
    side = lax.rem(me // 2, 2)
    mate = me + 1 - 2 * core
    across = me + 2 - 4 * side
    cross = across + 1 - 2 * core
    up, down = lax.rem(me + 4, n), lax.rem(me + n - 4, n)
    z_to = (1 - side) * down + side * up
    z_from = (1 - side) * up + side * down
    deck = me // 4
    edge = (deck == 0) | (deck == n // 4 - 1)
    owner = (core == side)
    giver = (core != side)

    load_taps = pltpu.make_async_copy(mf_hbm, mf, in_sem.at[2])
    load_taps.start()
    load_wave = pltpu.make_async_copy(wave, wave_v, in_sem.at[0])
    load_wave.start()
    load = pltpu.make_async_copy(rec, rec_v, in_sem.at[1])
    load.start()

    barrier = pltpu.get_barrier_semaphore()
    for other in (mate, across, cross, up, down):
        pl.semaphore_signal(barrier, inc=1, device_id={"shot": other}, device_id_type=MESH)
    pl.semaphore_wait(barrier, 5)

    def remote(src, dst, sem, target):
        return pltpu.make_async_remote_copy(
            src_ref=src, dst_ref=dst, send_sem=ssem.at[sem], recv_sem=rsem.at[sem],
            device_id={"shot": target}, device_id_type=MESH,
        )

    def block(src, dst, channel, i, target):
        rows = pl.ds(i * STEP, STEP)
        return remote(src.at[:, rows, :], dst.at[:, rows, :], channel * pieces + i, target)

    def x_copy(i):
        return block(wave, buf_c, CH_X, i, across)

    def z_copy(i):
        return block(wave, buf_z, CH_Z, i, z_to)

    def z_half(j):
        rows = pl.ds(early + j * HALF, HALF)
        return remote(wave.at[:, rows, :], buf_z.at[:, rows, :], CH_Z * pieces + last if j == 0 else 7 * pieces, z_to)

    def mate_copy(i):
        return block(wave, buf_m, CH_M, i, mate)

    def share(i):
        return block(buf_c, buf_d, CH_D, i, mate)

    def tile_a(i):
        return block(send_a, recv_a, CH_A, i, z_from)

    def corner(j):
        rows, cols = (
            (pl.ds(0, early), pl.ds(0, early)),
            (pl.ds(0, early), pl.ds(early, STEP)),
            (pl.ds(early, STEP), pl.ds(0, span)),
        )[j]
        return remote(
            send_c.at[:, rows, cols], recv_c.at[:, rows, cols], CH_C * pieces + j, across
        )

    def odd_x():
        rows = pl.ds(0, cut)
        return remote(send_x.at[:, rows, :], recv_x.at[:, rows, :], CH_O * pieces, cross)

    def odd_z(j):
        rows = pl.ds(cut, early - cut) if j == 0 else pl.ds(early, STEP)
        return remote(
            send_x.at[:, rows, :], recv_x.at[:, rows, :], CH_O * pieces + 1 + j, z_from
        )

    for i in range(pieces):
        x_copy(i).start()
        if i < last:
            z_copy(i).start()
    z_half(0).start()
    z_half(1).start()
    for i in range(pieces):
        mate_copy(i).start()

    load_taps.wait()
    width = taps_row.shape[1]
    taps_row[...] = jnp.zeros_like(taps_row)
    taps_row[0:2, 0:mf.shape[1]] = mf[...].astype(F32)
    row_id = lax.broadcasted_iota(jnp.int32, (span, width), 0)
    banded = []
    for c in range(2):
        x = jnp.broadcast_to(taps_row[c:c + 1, :], (span, width))
        x = pltpu.roll(x, width - half, 1)
        bit = 1
        while bit < span:
            x = jnp.where((row_id // bit) % 2 == 1, pltpu.roll(x, bit, 1), x)
            bit *= 2
        banded.append(x[:, :span].astype(BF16))
    for j in range(pieces):
        a = banded[0][j * STEP:(j + 1) * STEP]
        b = banded[1][j * STEP:(j + 1) * STEP]
        at = 2 * j * STEP
        weights[0, at:at + STEP, :] = a
        weights[0, at + STEP:at + 2 * STEP, :] = b
        weights[1, at:at + STEP, :] = -b
        weights[1, at + STEP:at + 2 * STEP, :] = a

    def product(left, start, count, right, k):
        a = left[:, start:start + count, :].reshape(2 * count, depth)
        b = right[:, k * STEP:(k + 1) * STEP, :].reshape(2 * STEP, depth)
        y = dot_t(a, b)
        top, low = y[:count], y[count:]
        return top[:, :STEP] - low[:, STEP:], top[:, STEP:] + low[:, :STEP]

    def keep(dst, pair, start, count, k):
        for c in range(2):
            dst[c, start:start + count, k * STEP:(k + 1) * STEP] = pair[c].astype(BF16)

    def flipped(dst, pair, k, skip=0):
        for c in range(2):
            dst[c, k * STEP + skip:(k + 1) * STEP, :] = pair[c].T[skip:].astype(BF16)

    def emit(t, k, src, start, count, j):
        rows = slice(start, start + count)
        for p in range(pieces):
            lo, hi = max(p - 1, 0) * STEP, min(p + 2, pieces) * STEP
            cols = slice(p * STEP, (p + 1) * STEP)
            f = sum(
                dot_t(src[c, rows, lo:hi], weights[c, 2 * p * STEP:2 * (p + 1) * STEP, lo:hi])
                for c in range(2)
            )
            out[t, k, 0, rows, cols] = (rec_v[t, k, 0, rows, cols].astype(F32) - f[:, :STEP]).astype(BF16)
            out[t, k, 1, rows, cols] = (rec_v[t, k, 1, rows, cols].astype(F32) - f[:, STEP:]).astype(BF16)

    load_wave.wait()
    for i in range(pieces):
        mate_copy(i).wait_recv()
        keep(tile_m, product(wave_v, 0, span, buf_m, i), 0, span, i)
    load.wait()
    emit(0, core, tile_m, 0, span, 0)

    for i in range(last):
        x_copy(i).wait_recv()
        share(i).start()
        keep(tile_c, product(wave_v, 0, span, buf_c, i), 0, span, i)
        z_copy(i).wait_recv()
        pair = product(wave_v, 0, span, buf_z, i)
        keep(tile_z, pair, 0, span, i)
        flipped(send_a, pair, i)
        pl.when(edge)(tile_a(i).start)
    for i in range(last):
        keep(send_c, product(buf_c, 0, early, buf_z, i), 0, early, i)
    corner(0).start()

    x_copy(last).wait_recv()
    share(last).start()
    z_half(0).wait_recv()

    @pl.when(jnp.logical_not(edge))
    def _():
        for i in range(last):
            tile_a(i).start()

    z_half(1).wait_recv()
    keep(send_c, product(buf_c, 0, early, buf_z, last), 0, early, last)
    corner(1).start()
    pair = product(wave_v, 0, span, buf_z, last)
    flipped(send_a, pair, last)
    tile_a(last).start()
    keep(tile_z, pair, 0, span, last)
    for i in range(pieces):
        keep(send_c, product(buf_c, early, STEP, buf_z, i), early, STEP, i)
    corner(2).start()

    for i in range(pieces):
        share(i).wait_recv()

    @pl.when(owner)
    def _():
        for i in range(pieces):
            pair = product(buf_d, 0, span, buf_z, i)
            for c in range(2):
                send_x[c, :cut, i * STEP:(i + 1) * STEP] = pair[c][:cut].astype(BF16)
            if (i + 1) * STEP > cut:
                flipped(send_x, pair, i, max(cut - i * STEP, 0))
        odd_x().start()
        odd_z(0).start()
        odd_z(1).start()

    keep(tile_c, product(wave_v, 0, span, buf_c, last), 0, span, last)
    emit(1, side, tile_c, 0, span, 1)
    emit(2, side, tile_z, 0, span, 2)

    @pl.when(giver)
    def _():
        for i in range(pieces):
            keep(tile_d, product(wave_v, 0, span, buf_d, i), 0, span, i)
        emit(0, 1 - core, tile_d, 0, span, 3)

    corner(0).wait_recv()
    corner(1).wait_recv()
    emit(1, 1 - side, recv_c, 0, early, 4)
    for i in range(last):
        tile_a(i).wait_recv()
        emit(2, 1 - side, recv_a, i * STEP, STEP, 6 + i)
    corner(2).wait_recv()
    emit(1, 1 - side, recv_c, early, STEP, 5)
    tile_a(last).wait_recv()
    emit(2, 1 - side, recv_a, early, STEP, 6 + last)

    @pl.when(owner)
    def _():
        odd_x().wait_recv()
        emit(0, 1 - core, recv_x, 0, cut, 3)
        odd_z(0).wait_recv()
        emit(0, 1 - core, recv_x, cut, early - cut, 6 + pieces)
        odd_z(1).wait_recv()
        emit(0, 1 - core, recv_x, early, STEP, 6 + pieces)
        odd_x().wait_send()
        odd_z(0).wait_send()
        odd_z(1).wait_send()
        pass
        pass

    for i in range(pieces):
        x_copy(i).wait_send()
        if i < last:
            z_copy(i).wait_send()
        mate_copy(i).wait_send()
        share(i).wait_send()
        tile_a(i).wait_send()
        pass
    z_half(0).wait_send()
    z_half(1).wait_send()
    for j in range(3):
        corner(j).wait_send()
    pass
    pass
    pass
    pass
    pass

    @pl.when(giver)
    def _():
        pass


def ladder(wavefield, recorded, match_filter):
    n = lax.axis_size("shot")
    _, span, depth = wavefield.shape
    pieces = span // STEP
    width = -(-(span + match_filter.shape[1]) // STEP) * STEP
    block = pltpu.VMEM((2, span, depth), BF16)
    flat = pltpu.VMEM((2, span, span), BF16)
    return pl.pallas_call(
        functools.partial(kernel, n),
        out_shape=jax.ShapeDtypeStruct(recorded.shape, recorded.dtype),
        in_specs=[
            pl.BlockSpec(memory_space=pltpu.HBM),
            pl.BlockSpec(memory_space=pltpu.HBM),
            pl.BlockSpec(memory_space=pltpu.HBM),
        ],
        out_specs=pl.BlockSpec(memory_space=pltpu.VMEM),
        scratch_shapes=[
            pltpu.VMEM(match_filter.shape, BF16),
            block,
            pltpu.VMEM((2, 2 * span, span), BF16),
            block, block, block, block,
            flat, flat, flat, flat, flat, flat, flat, flat, flat, flat,
            pltpu.VMEM(recorded.shape, BF16),
            pltpu.VMEM((8, width), F32),
            pltpu.SemaphoreType.DMA((7 * pieces + 1,)),
            pltpu.SemaphoreType.DMA((7 * pieces + 1,)),
            pltpu.SemaphoreType.DMA((3,)),
        ],
        compiler_params=pltpu.CompilerParams(
            collective_id=0, has_side_effects=True, vmem_limit_bytes=LIMIT
        ),
    )(*(pltpu.with_memory_space_constraint(x, pltpu.HBM) for x in (match_filter, wavefield, recorded)))


def passed_along(value, axis, steps):
    count = lax.axis_size(axis)
    pairs = [(source, (source + steps) % count) for source in range(count)]
    return lax.ppermute(value, axis, pairs)


def toeplitz(match_filter, block_span_width):
    tap_count = match_filter.shape[1]
    half_taps = (tap_count - 1) // 2
    row_index = lax.broadcasted_iota(jnp.int32, (block_span_width, block_span_width), 0)
    col_index = lax.broadcasted_iota(jnp.int32, (block_span_width, block_span_width), 1)
    lag_index = row_index - col_index + half_taps
    coeffs = match_filter.astype(jnp.float32)

    def place_tap(tap_index, carried):
        column = lax.dynamic_slice_in_dim(coeffs, tap_index, 1, 1)
        return jnp.where((lag_index == tap_index)[None], column[:, :, None], carried)

    return lax.fori_loop(
        0, tap_count, place_tap, jnp.zeros((2, block_span_width, block_span_width), jnp.float32)
    )


def filter_weights(match_filter, block_span_width):
    toe_pair = toeplitz(match_filter, block_span_width)
    real_component = toe_pair[0].astype(jnp.bfloat16)
    imag_part = toe_pair[1].astype(jnp.bfloat16)
    return jnp.stack(
        [jnp.stack([real_component, imag_part], 1), jnp.stack([-imag_part, real_component], 1)], 0
    )


def shards(wavefield, recorded, match_filter):
    cycle_size = lax.axis_size("shot")
    doubling = cycle_size // 8 == 2 and cycle_size // 4 == 4
    span, taps = wavefield.shape[1], match_filter.shape[1]
    tiled = span % STEP == 0 and span // STEP >= 3 and taps <= 2 * STEP and span % 32 == 0
    if doubling and cycle_size % 4 == 0 and tiled:
        return ladder(wavefield, recorded, match_filter)
    block_span_width = wavefield.shape[1]
    weights = filter_weights(match_filter, block_span_width)
    real_component = wavefield[0]
    imag_part = wavefield[1]
    left_rows = jnp.concatenate(
        [
            jnp.concatenate([real_component, -imag_part], 1),
            jnp.concatenate([imag_part, real_component], 1),
        ],
        0,
    )
    results = []
    for slot_index, offset in enumerate((1, cycle_size // 8, cycle_size // 4)):
        ahead_data = passed_along(wavefield, "shot", -offset)
        right_rows = jnp.concatenate([ahead_data[0], ahead_data[1]], 1)
        stacked = lax.dot_general(
            left_rows, right_rows, (((1,), (1,)), ((), ())), preferred_element_type=jnp.float32
        )
        forward_tile = stacked.astype(jnp.bfloat16).reshape(2, block_span_width, block_span_width)
        ahead_filtered = jnp.einsum(
            "csq,cqdx->dsx", forward_tile, weights, preferred_element_type=jnp.float32
        )
        received = passed_along(forward_tile, "shot", offset)
        behind_filtered = jnp.einsum(
            "csr,csdx->drx", received, weights, preferred_element_type=jnp.float32
        )
        ahead_out = (recorded[slot_index, 0].astype(jnp.float32) - ahead_filtered).astype(
            jnp.bfloat16
        )
        behind_out = (recorded[slot_index, 1].astype(jnp.float32) - behind_filtered).astype(
            jnp.bfloat16
        )
        results.append(jnp.stack([ahead_out, behind_out]))
    return jnp.stack(results)


def solution(mesh):
    return jax.shard_map(
        shards,
        mesh=mesh,
        in_specs=(P("freq", "shot", None), P("freq", None, None, "shot", None), P()),
        out_specs=P("freq", None, None, "shot", None),
        check_vma=False,
    )
```
